32 devices in a mesh: grp: 2 (over x), seq: 8 (over z, y), head: 2 (over core).
Axes of the slice: x: 2, y: 2, z: 4, core: 2. Of those that a mesh axis runs over, the one named last changes fastest.
Arguments:
- queries: bfloat16 [2048, 1280], P(('grp', 'seq'), 'head'), parts along dimension 0, may hold values from -6 to 6
- key_vectors: bfloat16 [2048, 1280], P(('grp', 'seq'), 'head'), parts along dimension 0, may hold values from -6 to 6
- value_vectors: bfloat16 [2048, 1280], P(('grp', 'seq'), 'head'), parts along dimension 0, may hold values from -6 to 6
- out_grad: bfloat16 [2048, 1280], P(('grp', 'seq'), 'head'), parts along dimension 0, may hold values from -48 to 48
- block_list: int32 [32, 8], P(('grp', 'seq')), parts along dimension 0, may hold values from 0 to 15, as said below
Outputs:
- grad_queries: bfloat16 [2048, 1280], P(('grp', 'seq'), 'head'), parts along dimension 0
- grad_keys: bfloat16 [2048, 1280], P(('grp', 'seq'), 'head'), parts along dimension 0
- grad_values: bfloat16 [2048, 1280], P(('grp', 'seq'), 'head'), parts along dimension 0
The draws below stay inside these ranges and needn't reach their ends.
There are 2 independent parts, one for each index of `grp`. The reference program is written for one: setup_inputs(seed, part) draws one part's arguments, and reference() takes and returns one part's arrays. A program takes and returns all parts, laid end to end along the dimension named above; each array names one. Nothing has to cross between parts.
Inputs may be any that keep to these rules, and one draw needn't show every extreme that they name: `block_list`: row g lists 8 different blocks; its first entry is g; every other entry is (g + o) modulo 16 with an offset o such that 1 <= |o| <= 4. In every row g with g % 8 == 0 both offsets 2 * 2 and -4 occur.
All inputs are finite; a program needn't handle non-finite values.
Results may differ from the reference program's by a relative error of at most 0.0097.
Values may be sent and summed in bfloat16 or wider, within the bound.
No kernel may reach another device: no remote copies, remote signals or barrier semaphores. Data moves between devices by JAX's collectives and lax.ppermute only.
A program may use at most 64 MiB of HBM per device.

```python
import jax
import jax.numpy as jnp
from jax import lax

HEADS = 10
DH = 128
BLOCK = 64
NSEL = 8
BLK_DEV = 2
TOKENS = 1024
NB = 16
N_SEQ = 8


def drawn_field(key, salt):
    sub_key = jax.random.fold_in(key, salt)
    return jnp.clip(jax.random.normal(sub_key, (TOKENS, HEADS * DH), jnp.float32), -6.0, 6.0)


def draw_queries(key, part):
    field = drawn_field(key, 1)
    return field.astype(jnp.bfloat16)


def draw_key_vectors(key, part):
    field = drawn_field(key, 2)
    return field.astype(jnp.bfloat16)


def draw_block_list(key, part):
    neighbourhood_span = 2 * BLK_DEV
    near_reach = max(4, BLK_DEV // 2)
    magnitudes = jnp.arange(1, neighbourhood_span + 1, dtype=jnp.int32)
    valid = (magnitudes <= near_reach) | (magnitudes % 2 == 0) & (magnitudes <= BLK_DEV) | (magnitudes % 4 == 0)
    spacing_strides = jnp.concatenate([magnitudes, -magnitudes])
    pairwise_allowed_filter = jnp.concatenate([valid, valid])
    tile_total = 2 * neighbourhood_span
    noise_perturbation = jax.random.randint(key, (NB, tile_total), 0, 1 << 20, dtype=jnp.int32)
    sequence_positions = jnp.arange(NB, dtype=jnp.int32)[:, None]
    affinity_increment = jnp.where((sequence_positions % 8 == 0) & (jnp.abs(spacing_strides)[None, :] == neighbourhood_span), 1 << 28, 0).astype(jnp.int32)
    raw_affinity = jnp.where(pairwise_allowed_filter[None, :], noise_perturbation * tile_total + jnp.arange(tile_total, dtype=jnp.int32)[None, :] + affinity_increment, -1)
    top_values, picks = lax.top_k(raw_affinity, NSEL - 1)
    chosen_offsets = spacing_strides[picks]
    key_blocks = jnp.mod(sequence_positions + chosen_offsets, NB)
    return jnp.concatenate([sequence_positions, key_blocks], axis=1).astype(jnp.int32)


def block_levels(own_key, shape, cuts, low, high):
    def one(dim, parts):
        draws = jax.random.uniform(jax.random.fold_in(jax.random.fold_in(own_key, 6), dim), (parts,), jnp.float32, low / len(cuts), high / len(cuts))
        return jnp.repeat(jnp.exp(draws), shape[dim] // parts).reshape((-1,) + (1,) * (len(shape) - dim - 1))

    level = one(*cuts[0])
    for cut in cuts[1:]:
        level = level * one(*cut)
    return level


def centred(rng, extent, deviation, most, pieces=(), kind=jnp.bfloat16):
    loudness = block_levels(rng, extent, pieces, -0.22, 0.18) if pieces else 1.0
    array = jax.random.normal(rng, extent, jnp.float32) * deviation * loudness
    return jnp.minimum(jnp.maximum(array, -most), most).astype(kind)


def setup_inputs(seed: int = 0, part: int = 0) -> dict:
    seeds = jax.random.split(jax.random.key(seed), 6)
    own_keys = jax.random.split(jax.random.fold_in(seeds[5], part), 6)
    return {
        "queries": draw_queries(jax.random.fold_in(jax.random.fold_in(seeds[5], part), 71), part),
        "key_vectors": draw_key_vectors(jax.random.fold_in(jax.random.fold_in(seeds[5], part), 71), part),
        "value_vectors": centred(own_keys[2], (TOKENS, HEADS * DH), 1.0, 6.0, ((0, 8), (1, 2))),
        "out_grad": centred(own_keys[3], (TOKENS, HEADS * DH), 8.0, 48.0, ((0, 8), (1, 2))),
        "block_list": draw_block_list(jax.random.fold_in(jax.random.fold_in(seeds[5], part), 71), part),
    }


def reference(queries, key_vectors, value_vectors, out_grad, block_list):
    score_scale = DH ** -0.5
    block_shape = (NB, BLOCK, HEADS, DH)
    query_all = queries.astype(jnp.float32).reshape(block_shape)
    key_all = key_vectors.astype(jnp.float32).reshape(block_shape)
    value_all = value_vectors.astype(jnp.float32).reshape(block_shape)
    grad_all = out_grad.astype(jnp.float32).reshape(block_shape)
    window_blocks = 5 * BLK_DEV

    def shard_step(carry, shard):
        acc_keys, acc_values = carry
        start = shard * BLK_DEV
        rows_list = lax.dynamic_slice_in_dim(block_list, start, BLK_DEV, 0)
        query_rows = lax.dynamic_slice_in_dim(query_all, start, BLK_DEV, 0)
        grad_rows = lax.dynamic_slice_in_dim(grad_all, start, BLK_DEV, 0)
        key_flat = key_all[rows_list].reshape(BLK_DEV, NSEL * BLOCK, HEADS, DH)
        value_flat = value_all[rows_list].reshape(BLK_DEV, NSEL * BLOCK, HEADS, DH)
        scores = jnp.einsum('bqhd,bmhd->bhqm', query_rows, key_flat) * score_scale
        top_score = jnp.max(scores, axis=-1, keepdims=True)
        expo = jnp.exp(scores - top_score)
        probs = expo / jnp.sum(expo, axis=-1, keepdims=True)
        probability_lower = lax.optimization_barrier(probs.astype(jnp.bfloat16)).astype(jnp.float32)
        attended = jnp.einsum('bhqm,bmhd->bqhd', probability_lower, value_flat)
        delta = jnp.sum(grad_rows * attended, axis=-1)
        grad_probs = jnp.einsum('bqhd,bmhd->bhqm', grad_rows, value_flat)
        grad_scores = probs * (grad_probs - jnp.transpose(delta, (0, 2, 1))[..., None])
        gradient_lower = lax.optimization_barrier(grad_scores.astype(jnp.bfloat16)).astype(jnp.float32)
        grad_query = (score_scale * jnp.einsum('bhqm,bmhd->bqhd', gradient_lower, key_flat)).astype(jnp.bfloat16)
        value_pairs = jnp.einsum('bhqm,bqhd->bmhd', probability_lower, grad_rows).reshape(BLK_DEV * NSEL, BLOCK, HEADS, DH)
        key_pairs = (score_scale * jnp.einsum('bhqm,bqhd->bmhd', gradient_lower, query_rows)).reshape(BLK_DEV * NSEL, BLOCK, HEADS, DH)
        local_ids = jnp.mod(rows_list - (shard - 2) * BLK_DEV, NB).reshape(-1).astype(jnp.int32)
        key_window = jax.ops.segment_sum(key_pairs, local_ids, num_segments=window_blocks)
        value_window = jax.ops.segment_sum(value_pairs, local_ids, num_segments=window_blocks)
        key_window = lax.optimization_barrier(key_window.astype(jnp.bfloat16)).astype(jnp.float32)
        value_window = lax.optimization_barrier(value_window.astype(jnp.bfloat16)).astype(jnp.float32)
        window_ids = jnp.mod((shard - 2) * BLK_DEV + jnp.arange(window_blocks, dtype=jnp.int32), NB).astype(jnp.int32)
        acc_keys = acc_keys.at[window_ids].add(key_window)
        acc_values = acc_values.at[window_ids].add(value_window)
        return (acc_keys, acc_values), grad_query

    zeros_init = jnp.zeros(block_shape, jnp.float32)
    (acc_keys, acc_values), grad_query = lax.scan(shard_step, (zeros_init, zeros_init), jnp.arange(N_SEQ, dtype=jnp.int32))
    grad_queries = grad_query.reshape(TOKENS, HEADS * DH)
    grad_keys = acc_keys.astype(jnp.bfloat16).reshape(TOKENS, HEADS * DH)
    grad_values = acc_values.astype(jnp.bfloat16).reshape(TOKENS, HEADS * DH)
    return (grad_queries, grad_keys, grad_values)
```

```python
import functools

import jax
import jax.numpy as jnp
from jax import lax
from jax.experimental import pallas as pl
from jax.experimental.pallas import tpu as pltpu
from jax.sharding import PartitionSpec as P

DH = 128
NEG = -1e30
SLOTS = 5
VMEM = pl.BlockSpec(memory_space=pltpu.VMEM)


def permuted(x, kind):
    n = lax.axis_size("seq")
    toward = {"partner": 1, "far_up": 2, "far_down": -2}[kind]
    route = [((i + (toward if i % 2 == 0 else -toward)) % n, i) for i in range(n)]
    return lax.ppermute(x, "seq", route)


def nt(a, b):
    return lax.dot_general(a, b, (((1,), (1,)), ((), ())), preferred_element_type=jnp.float32)


def nn(a, b):
    return lax.dot_general(a, b, (((1,), (0,)), ((), ())), preferred_element_type=jnp.float32)


def tn(a, b):
    return lax.dot_general(a, b, (((0,), (0,)), ((), ())), preferred_element_type=jnp.float32)


def masked(scores, bias_ref, row, block):
    parts = [
        scores[b * block : (b + 1) * block, :] + bias_ref[row + b : row + b + 1, :]
        for b in range(scores.shape[0] // block)
    ]
    return jnp.concatenate(parts, axis=0)


def query_kernel(heads, blk_dev, q_ref, g_ref, bias_ref, *refs):
    kv_refs, (dq_ref, stat_ref, dk_ref, dv_ref) = refs[:SLOTS], refs[SLOTS:]
    tok = q_ref.shape[0]
    block = tok // blk_dev
    scale = DH ** (-0.5)
    stat_ref[...] = jnp.zeros_like(stat_ref)
    stat_ref[2 * heads : 2 * heads + SLOTS * blk_dev, :] = bias_ref[...]
    for h in range(heads):
        cols = slice(h * DH, (h + 1) * DH)
        q, g = q_ref[:, cols], g_ref[:, cols]
        ks = [r[:tok, cols] for r in kv_refs]
        vs = [r[tok:, cols] for r in kv_refs]
        scores = [
            masked(nt(k, q) * scale, bias_ref, s * blk_dev, block) for s, k in enumerate(ks)
        ]
        top = functools.reduce(jnp.maximum, scores).max(axis=0, keepdims=True)
        expo = [jnp.exp(s - top) for s in scores]
        total = functools.reduce(jnp.add, expo).sum(axis=0, keepdims=True)
        inv = 1.0 / total
        probs = [e * inv for e in expo]
        low = [p.astype(jnp.bfloat16) for p in probs]
        grad_probs = [nt(v, g) for v in vs]
        delta = functools.reduce(
            jnp.add, [p.astype(jnp.float32) * d for p, d in zip(low, grad_probs)]
        ).sum(axis=0, keepdims=True)
        ds = [(p * (d - delta)).astype(jnp.bfloat16) for p, d in zip(probs, grad_probs)]
        dq = functools.reduce(jnp.add, [tn(d, k) for d, k in zip(ds, ks)])
        dq_ref[:, cols] = (dq * scale).astype(jnp.bfloat16)
        stat_ref[h : h + 1, :] = top + jnp.log(total)
        stat_ref[heads + h : heads + h + 1, :] = delta
        dk_ref[:, cols] = nn(ds[0], q)
        dv_ref[:, cols] = nn(low[0], g)


def key_kernel(heads, blk_dev, rows, last, kv_ref, dk_in, dv_in, *refs):
    count = len(rows)
    qg_refs, stat_refs, (dk_ref, dv_ref) = refs[:count], refs[count : 2 * count], refs[2 * count :]
    tok = kv_ref.shape[0] // 2
    block = tok // blk_dev
    scale = DH ** (-0.5)
    for h in range(heads):
        cols = slice(h * DH, (h + 1) * DH)
        k, v = kv_ref[:tok, cols], kv_ref[tok:, cols]
        dk, dv = dk_in[:, cols], dv_in[:, cols]
        for qg, stat, row in zip(qg_refs, stat_refs, rows):
            q, g = qg[:tok, cols], qg[tok:, cols]
            scores = masked(nt(k, q) * scale, stat, 2 * heads + row * blk_dev, block)
            probs = jnp.exp(scores - stat[h : h + 1, :])
            ds = (probs * (nt(v, g) - stat[heads + h : heads + h + 1, :])).astype(jnp.bfloat16)
            dk = dk + nn(ds, q)
            dv = dv + nn(probs.astype(jnp.bfloat16), g)
        if last:
            dk_ref[:, cols] = (dk * scale).astype(jnp.bfloat16)
            dv_ref[:, cols] = dv.astype(jnp.bfloat16)
        else:
            dk_ref[:, cols] = dk
            dv_ref[:, cols] = dv


def key_call(heads, blk_dev, rows, last, kv, dk, dv, qgs, stats):
    dtype = jnp.bfloat16 if last else jnp.float32
    out = jax.ShapeDtypeStruct(dk.shape, dtype)
    pairs = len(rows) * heads * dk.shape[0] ** 2
    return pl.pallas_call(
        functools.partial(key_kernel, heads, blk_dev, rows, last),
        out_shape=(out, out),
        in_specs=[VMEM] * (3 + 2 * len(rows)),
        out_specs=(VMEM, VMEM),
        cost_estimate=pl.CostEstimate(
            flops=8 * pairs * DH, bytes_accessed=4 * dk.size * 4, transcendentals=pairs
        ),
        name="key_side_last" if last else "key_side",
    )(kv, dk, dv, *qgs, *stats)


def per_device(queries, key_vectors, value_vectors, out_grad, block_list):
    tok_dev, feat_width = queries.shape
    blk_dev, list_len = block_list.shape
    block_rows = tok_dev // blk_dev
    heads = feat_width // DH
    seq_count = lax.axis_size("seq")
    seq_index = lax.axis_index("seq")

    kv = jnp.concatenate([key_vectors, value_vectors], axis=0)
    qg = jnp.concatenate([queries, out_grad], axis=0)
    kv_up = permuted(kv, "far_up")
    kv_partner = permuted(kv, "partner")
    kv_down = permuted(kv, "far_down")
    kv_relay = permuted(kv_up, "partner")
    qg_up = permuted(qg, "far_up")
    qg_partner = permuted(qg, "partner")
    qg_down = permuted(qg, "far_down")
    qg_relay = permuted(qg_up, "partner")

    side = 1 - 2 * (seq_index % 2)
    shards = seq_index + side * jnp.array([0, 1, -1, 2, -2], jnp.int32)
    blocks = shards[:, None] * blk_dev + jnp.arange(blk_dev, dtype=jnp.int32)[None, :]
    blocks = jnp.mod(blocks, seq_count * blk_dev).reshape(-1)
    listed = (block_list[None, :, :] == blocks[:, None, None]).any(axis=-1)
    bias = jnp.repeat(jnp.where(listed, 0.0, NEG).astype(jnp.float32), block_rows, axis=1)

    rows = 2 * heads + SLOTS * blk_dev
    stat_shape = (-(-rows // 8) * 8, tok_dev)
    f32_out = jax.ShapeDtypeStruct((tok_dev, feat_width), jnp.float32)
    pairs = SLOTS * heads * tok_dev * tok_dev
    grad_queries, stats, dk, dv = pl.pallas_call(
        functools.partial(query_kernel, heads, blk_dev),
        out_shape=(
            jax.ShapeDtypeStruct((tok_dev, feat_width), jnp.bfloat16),
            jax.ShapeDtypeStruct(stat_shape, jnp.float32),
            f32_out,
            f32_out,
        ),
        in_specs=[VMEM] * (3 + SLOTS),
        out_specs=(VMEM,) * 4,
        cost_estimate=pl.CostEstimate(
            flops=7 * pairs * DH, bytes_accessed=12 * kv.size, transcendentals=pairs
        ),
        name="query_side",
    )(queries, out_grad, bias, kv, kv_partner, kv_relay, kv_up, kv_down)

    stats_up = permuted(stats, "far_up")
    stats_partner = permuted(stats, "partner")
    stats_down = permuted(stats, "far_down")
    stats_relay = permuted(stats_up, "partner")

    dk, dv = key_call(
        heads, blk_dev, (1, 4), False, kv, dk, dv, (qg_partner, qg_up), (stats_partner, stats_up)
    )
    grad_keys, grad_values = key_call(
        heads, blk_dev, (3, 2), True, kv, dk, dv, (qg_down, qg_relay), (stats_down, stats_relay)
    )
    return grad_queries, grad_keys, grad_values


def solution(mesh):
    spec = P(("grp", "seq"), "head")
    return jax.shard_map(
        per_device,
        mesh=mesh,
        in_specs=(spec, spec, spec, spec, P(("grp", "seq"), None)),
        out_specs=(spec, spec, spec),
        check_vma=False,
    )
```

```python
import functools

import jax
import jax.numpy as jnp
from jax import lax
from jax.experimental import pallas as pl
from jax.experimental.pallas import tpu as pltpu
from jax.sharding import PartitionSpec as P

DH = 128
NEG = -1e30
VMEM_GRANT = 16 * 2**20
SLOTS = 5
VMEM = pl.BlockSpec(memory_space=pltpu.VMEM)


def permuted(x, kind, name):
    n = lax.axis_size("seq")
    toward = {"partner": 1, "far_up": 2, "far_down": -2}[kind]
    route = [((i + (toward if i % 2 == 0 else -toward)) % n, i) for i in range(n)]
    with jax.named_scope(name):
        return lax.ppermute(x, "seq", route)


def nt(a, b):
    return lax.dot_general(a, b, (((1,), (1,)), ((), ())), preferred_element_type=jnp.float32)


def nn(a, b):
    return lax.dot_general(a, b, (((1,), (0,)), ((), ())), preferred_element_type=jnp.float32)


def tn(a, b):
    return lax.dot_general(a, b, (((0,), (0,)), ((), ())), preferred_element_type=jnp.float32)


def masked(scores, bias_ref, row, block):
    parts = [
        scores[b * block : (b + 1) * block, :] + bias_ref[row + b : row + b + 1, :]
        for b in range(scores.shape[0] // block)
    ]
    return jnp.concatenate(parts, axis=0)


def query_kernel(heads, blk_dev, q_ref, g_ref, bias_ref, *refs):
    kv_refs, (dq_ref, stat_ref, dk_ref, dv_ref) = refs[:SLOTS], refs[SLOTS:]
    tok = q_ref.shape[0]
    block = tok // blk_dev
    scale = DH ** (-0.5)
    stat_ref[...] = jnp.zeros_like(stat_ref)
    stat_ref[2 * heads : 2 * heads + SLOTS * blk_dev, :] = bias_ref[...]
    for h in range(heads):
        cols = slice(h * DH, (h + 1) * DH)
        q, g = q_ref[:, cols], g_ref[:, cols]
        ks = [r[:tok, cols] for r in kv_refs]
        vs = [r[tok:, cols] for r in kv_refs]
        scores = [
            masked(nt(k, q) * scale, bias_ref, s * blk_dev, block) for s, k in enumerate(ks)
        ]
        top = functools.reduce(jnp.maximum, scores).max(axis=0, keepdims=True)
        expo = [jnp.exp(s - top) for s in scores]
        total = functools.reduce(jnp.add, expo).sum(axis=0, keepdims=True)
        inv = 1.0 / total
        probs = [e * inv for e in expo]
        low = [p.astype(jnp.bfloat16) for p in probs]
        grad_probs = [nt(v, g) for v in vs]
        delta = functools.reduce(
            jnp.add, [p.astype(jnp.float32) * d for p, d in zip(low, grad_probs)]
        ).sum(axis=0, keepdims=True)
        ds = [(p * (d - delta)).astype(jnp.bfloat16) for p, d in zip(probs, grad_probs)]
        dq = functools.reduce(jnp.add, [tn(d, k) for d, k in zip(ds, ks)])
        dq_ref[:, cols] = (dq * scale).astype(jnp.bfloat16)
        stat_ref[h : h + 1, :] = top + jnp.log(total)
        stat_ref[heads + h : heads + h + 1, :] = delta
        dk_ref[:, cols] = nn(ds[0], q)
        dv_ref[:, cols] = nn(low[0], g)


def key_kernel(heads, blk_dev, rows, last, kv_ref, dk_in, dv_in, *refs):
    count = len(rows)
    qg_refs, stat_refs, (dk_ref, dv_ref) = refs[:count], refs[count : 2 * count], refs[2 * count :]
    tok = kv_ref.shape[0] // 2
    block = tok // blk_dev
    scale = DH ** (-0.5)
    for h in range(heads):
        cols = slice(h * DH, (h + 1) * DH)
        k, v = kv_ref[:tok, cols], kv_ref[tok:, cols]
        dk, dv = dk_in[:, cols], dv_in[:, cols]
        for qg, stat, row in zip(qg_refs, stat_refs, rows):
            q, g = qg[:tok, cols], qg[tok:, cols]
            scores = masked(nt(k, q) * scale, stat, 2 * heads + row * blk_dev, block)
            probs = jnp.exp(scores - stat[h : h + 1, :])
            ds = (probs * (nt(v, g) - stat[heads + h : heads + h + 1, :])).astype(jnp.bfloat16)
            dk = dk + nn(ds, q)
            dv = dv + nn(probs.astype(jnp.bfloat16), g)
        if last:
            dk_ref[:, cols] = (dk * scale).astype(jnp.bfloat16)
            dv_ref[:, cols] = dv.astype(jnp.bfloat16)
        else:
            dk_ref[:, cols] = dk
            dv_ref[:, cols] = dv


def key_call(heads, blk_dev, rows, last, kv, dk, dv, qgs, stats):
    dtype = jnp.bfloat16 if last else jnp.float32
    out = jax.ShapeDtypeStruct(dk.shape, dtype)
    pairs = len(rows) * heads * dk.shape[0] ** 2
    return pl.pallas_call(
        functools.partial(key_kernel, heads, blk_dev, rows, last),
        out_shape=(out, out),
        in_specs=[VMEM] * (3 + 2 * len(rows)),
        out_specs=(VMEM, VMEM),
        compiler_params=pltpu.CompilerParams(vmem_limit_bytes=VMEM_GRANT),
        cost_estimate=pl.CostEstimate(
            flops=8 * pairs * DH, bytes_accessed=4 * dk.size * 4, transcendentals=pairs
        ),
        name="key_side_last" if last else "key_side",
    )(kv, dk, dv, *qgs, *stats)


def per_device(queries, key_vectors, value_vectors, out_grad, block_list):
    tok_dev, feat_width = queries.shape
    blk_dev, list_len = block_list.shape
    block_rows = tok_dev // blk_dev
    heads = feat_width // DH
    seq_count = lax.axis_size("seq")
    seq_index = lax.axis_index("seq")

    kv = jnp.concatenate([key_vectors, value_vectors], axis=0)
    qg = jnp.concatenate([queries, out_grad], axis=0)
    kv_up = permuted(kv, "far_up", "kv_up")
    kv_partner = permuted(kv, "partner", "kv_partner")
    kv_down = permuted(kv, "far_down", "kv_down")
    kv_relay = permuted(kv_up, "partner", "kv_relay")
    qg_up = permuted(qg, "far_up", "qg_up")
    qg_partner = permuted(qg, "partner", "qg_partner")
    qg_down = permuted(qg, "far_down", "qg_down")
    qg_relay = permuted(qg_up, "partner", "qg_relay")

    side = 1 - 2 * (seq_index % 2)
    shards = seq_index + side * jnp.array([0, 1, -1, 2, -2], jnp.int32)
    blocks = shards[:, None] * blk_dev + jnp.arange(blk_dev, dtype=jnp.int32)[None, :]
    blocks = jnp.mod(blocks, seq_count * blk_dev).reshape(-1)
    listed = (block_list[None, :, :] == blocks[:, None, None]).any(axis=-1)
    bias = jnp.repeat(jnp.where(listed, 0.0, NEG).astype(jnp.float32), block_rows, axis=1)

    rows = 2 * heads + SLOTS * blk_dev
    stat_shape = (-(-rows // 8) * 8, tok_dev)
    f32_out = jax.ShapeDtypeStruct((tok_dev, feat_width), jnp.float32)
    pairs = SLOTS * heads * tok_dev * tok_dev
    grad_queries, stats, dk, dv = pl.pallas_call(
        functools.partial(query_kernel, heads, blk_dev),
        out_shape=(
            jax.ShapeDtypeStruct((tok_dev, feat_width), jnp.bfloat16),
            jax.ShapeDtypeStruct(stat_shape, jnp.float32),
            f32_out,
            f32_out,
        ),
        in_specs=[VMEM] * (3 + SLOTS),
        out_specs=(VMEM,) * 4,
        compiler_params=pltpu.CompilerParams(vmem_limit_bytes=VMEM_GRANT),
        cost_estimate=pl.CostEstimate(
            flops=7 * pairs * DH, bytes_accessed=12 * kv.size, transcendentals=pairs
        ),
        name="query_side",
    )(queries, out_grad, bias, kv, kv_partner, kv_relay, kv_up, kv_down)

    stats_up = permuted(stats, "far_up", "st_up")
    stats_partner = permuted(stats, "partner", "st_partner")
    stats_down = permuted(stats, "far_down", "st_down")
    stats_relay = permuted(stats_up, "partner", "st_relay")

    dk, dv = key_call(
        heads, blk_dev, (1, 4), False, kv, dk, dv, (qg_partner, qg_up), (stats_partner, stats_up)
    )
    grad_keys, grad_values = key_call(
        heads, blk_dev, (3, 2), True, kv, dk, dv, (qg_down, qg_relay), (stats_down, stats_relay)
    )
    return grad_queries, grad_keys, grad_values


def solution(mesh):
    spec = P(("grp", "seq"), "head")
    return jax.shard_map(
        per_device,
        mesh=mesh,
        in_specs=(spec, spec, spec, spec, P(("grp", "seq"), None)),
        out_specs=(spec, spec, spec),
        check_vma=False,
    )
```
